512 devices in a mesh: row: 8 (over z_hi, core), col: 16 (over y, z_lo), depth: 4 (over x).
Axes of the slice: x: 4, y: 4, z: 16 (z_hi: 4, z_lo: 4; z = z_hi * 4 + z_lo), core: 2. Of those that a mesh axis runs over, the one named last changes fastest.
Arguments:
- values: bfloat16 [768, 16, 128, 128], P(('row', 'col')), may hold values from -0.47851562 to 0.47851562
- columns: int32 [768, 16], replicated, may hold values from 0 to 767, as said below
Outputs:
- purified: bfloat16 [768, 16, 128, 128], P(('row', 'col'), 'depth')
The draws below stay inside these ranges and needn't reach their ends.
Inputs may be any that keep to these rules, and one draw needn't show every extreme that they name: Each block row a names 16 different block columns, a itself among them, all within 8 of a around the cycle of 768 block rows (indices wrap).
All inputs are finite; a program needn't handle non-finite values.
Results may differ from the reference program's by a relative error of at most 0.0047.
Values may be sent and summed in bfloat16 or wider, within the bound.
A program may use at most 128 MiB of HBM per device.

```python
import jax
import jax.numpy as jnp
from jax import lax

BS = 128
KB = 16
HB = 8
NB = 768


def draw_columns(key, part):
    own_key = jax.random.fold_in(key, 11)
    window = 2 * HB + 1
    scores = jax.random.randint(own_key, (NB, window), 0, 1 << 20)
    offsets = jnp.arange(window, dtype=jnp.int32) - HB
    scores = scores * window + jnp.arange(window, dtype=jnp.int32)[None, :]
    scores = jnp.where(offsets[None, :] == 0, 1 << 30, scores)
    top_values, picked = lax.top_k(scores, KB)
    row_ids = jnp.arange(NB, dtype=jnp.int32)[:, None]
    return jnp.mod(row_ids + picked.astype(jnp.int32) - HB, NB).astype(jnp.int32)


def steps_of(key, shape, pieces, least, high):
    loudness = 1.0
    for dim, blocks in pieces:
        draws = jax.random.uniform(jax.random.fold_in(jax.random.fold_in(key, 6), dim), (blocks,), jnp.float32, least / len(pieces), high / len(pieces))
        loudness = loudness * jnp.repeat(jnp.exp(draws), shape[dim] // blocks).reshape((-1,) + (1,) * (len(shape) - 1 - dim))
    return loudness


def normal_values(rng, dims, deviation, limit, cuts=(), held_as=jnp.bfloat16):
    array = deviation * jax.random.normal(rng, dims, jnp.float32)
    if cuts:
        array = array * steps_of(rng, dims, cuts, -0.22, 0.18)
    return jnp.clip(array, -limit, limit).astype(held_as)


def setup_inputs(seed: int = 0) -> dict:
    key_of = jax.random.split(jax.random.key(seed), 3)
    return {
        "values": normal_values(key_of[0], (NB, KB, BS, BS), 0.08, 0.47851562, ((0, 128),)),
        "columns": draw_columns(jax.random.fold_in(key_of[2], 71), 0),
    }


def selection(values, columns, row_cols):
    partner_cols = jnp.take(columns, row_cols, axis=0)
    same_column = partner_cols[:, None, :] == row_cols[None, :, None]
    slot_ids = jnp.arange(KB, dtype=jnp.int32)
    present = jnp.any(same_column, axis=2)
    chosen = jnp.sum(jnp.where(same_column, slot_ids[None, None, :], 0), axis=2).astype(jnp.int32)
    row_blocks = jnp.take(values, row_cols, axis=0).reshape(KB * KB, BS, BS)
    flat_index = (slot_ids[:, None] * KB + chosen).astype(jnp.int32)
    picked = jnp.take(row_blocks, flat_index, axis=0)
    return jnp.where(present[:, :, None, None], picked, jnp.zeros((), picked.dtype))


def reference(values, columns):
    row_ids = jnp.arange(NB, dtype=jnp.int32)

    def square_row(block_row):
        chosen_blocks = selection(values, columns, columns[block_row])
        return jnp.einsum("ixy,ijyz->jxz", values[block_row].astype(jnp.float32), chosen_blocks.astype(jnp.float32))

    square32 = lax.map(square_row, row_ids)
    square = square32.astype(jnp.bfloat16)

    def purify_row(block_row):
        chosen_blocks = selection(values, columns, columns[block_row])
        cube_row = jnp.einsum("ixy,ijyz->jxz", square[block_row].astype(jnp.float32), chosen_blocks.astype(jnp.float32))
        return (3.0 * square32[block_row] - 2.0 * cube_row).astype(jnp.bfloat16)

    return lax.map(purify_row, row_ids)
```

```python
import functools

import jax
import jax.numpy as jnp
from jax import lax
from jax.experimental import pallas as pl
from jax.experimental.pallas import tpu as pltpu
from jax.sharding import PartitionSpec as P

HB = 8
BAND = 2 * HB + 1
MESH = pl.DeviceIdType.MESH


def spread_kernel(off_ref, v_ref, o_ref):
    m = pl.program_id(0)
    slots, bs = v_ref.shape[1], v_ref.shape[2]
    o_ref[...] = jnp.zeros_like(o_ref)
    for s in range(slots):
        at = pl.multiple_of(off_ref[m, s] * bs, bs)
        o_ref[0, :, pl.ds(at, bs)] = v_ref[0, s]


def spread(off, values):
    rows, slots, bs, _ = values.shape
    return pl.pallas_call(
        spread_kernel,
        out_shape=jax.ShapeDtypeStruct((rows, bs, BAND * bs), values.dtype),
        grid_spec=pltpu.PrefetchScalarGridSpec(
            num_scalar_prefetch=1,
            grid=(rows,),
            in_specs=[pl.BlockSpec((1, slots, bs, bs), lambda m, off: (m, 0, 0, 0))],
            out_specs=pl.BlockSpec((1, bs, BAND * bs), lambda m, off: (m, 0, 0)),
        ),
    )(off, values)


def halo_rows(rows):
    frame = rows + 2 * HB
    listed = []
    for near in range(HB):
        for f in (HB - 1 - near, HB + rows + near):
            owner, m = (f - HB) // rows, (f - HB) % rows
            lo = max(0, HB - f)
            hi = min(2 * HB, frame - 1 + HB - f)
            listed.append((f, owner, m, lo, f + lo - HB, hi - lo + 1))
    return listed


def square_kernel(sizes, own_ref, field, square, own_sem, z_send, z_recv, x_send, x_recv, y_send, y_recv):
    nrow, ncol, layers = sizes
    rows, bs = own_ref.shape[0], own_ref.shape[1]
    frame = rows + 2 * HB
    groups = nrow * ncol
    strip = bs // layers
    half = strip // 2
    r, c, d = lax.axis_index("row"), lax.axis_index("col"), lax.axis_index("depth")
    g = r * ncol + c
    halo = halo_rows(rows)

    def group_at(by):
        t = lax.rem(g + by + groups, groups)
        return (lax.div(t, ncol), lax.rem(t, ncol), d)

    up, down = lax.rem(d + 1, layers), lax.rem(d + layers - 1, layers)
    beside = ((r, c, up), (r, c, down))
    owners = sorted({h[1] for h in halo})

    barrier = pltpu.get_barrier_semaphore()
    for by in owners:
        pl.semaphore_signal(barrier, inc=1, device_id=group_at(by), device_id_type=MESH)
    for peer in beside:
        pl.semaphore_signal(barrier, inc=1, device_id=peer, device_id_type=MESH)
    pl.semaphore_wait(barrier, len(owners) + 2)

    def part(k, layer, start, count):
        f, _, _, _, col, blocks = halo[k]
        first = pl.multiple_of(f * bs + layer * strip + start, half)
        return field.at[pl.ds(first, count), pl.ds(col * bs, blocks * bs)]

    def z_copy(k):
        f, owner, m, lo, col, blocks = halo[k]
        src = own_ref.at[m, pl.ds(pl.multiple_of(d * strip, strip), strip), pl.ds(lo * bs, blocks * bs)]
        return pltpu.make_async_remote_copy(
            src, part(k, d, 0, strip), z_send.at[k], z_recv.at[k], group_at(-owner), MESH
        )

    def x_copy(k, way):
        ref = part(k, d, 0, strip)
        return pltpu.make_async_remote_copy(ref, ref, x_send.at[way, k], x_recv.at[way, k], beside[way], MESH)

    def y_copy(k, way):
        ref = part(k, (down, up)[way], way * half, half)
        return pltpu.make_async_remote_copy(ref, ref, y_send.at[way, k], y_recv.at[way, k], beside[way], MESH)

    own_copies = [
        pltpu.make_async_copy(
            own_ref.at[m],
            field.at[pl.ds((HB + m) * bs, bs), pl.ds(m * bs, BAND * bs)],
            own_sem.at[m],
        )
        for m in range(rows)
    ]
    for k in range(len(halo)):
        z_copy(k).start()
    for copy in own_copies:
        copy.start()

    for f in range(frame):
        low, high = max(0, f - HB), min(frame, f + HB + 1)
        if low:
            field[pl.ds(f * bs, bs), pl.ds(0, low * bs)] = jnp.zeros((bs, low * bs), field.dtype)
        if high < frame:
            field[pl.ds(f * bs, bs), pl.ds(high * bs, (frame - high) * bs)] = jnp.zeros(
                (bs, (frame - high) * bs), field.dtype
            )
    square[...] = jnp.zeros_like(square)

    def add_pair(f):
        a0, a1 = max(0, f - 2 * HB), min(rows, f + 2)
        c0, c1 = max(0, f - HB), min(frame, f + HB + 2)
        left = field[pl.ds((HB + a0) * bs, (a1 - a0) * bs), pl.ds(f * bs, 2 * bs)]

        def body(t, _):
            at = pl.multiple_of((c0 + 2 * t) * bs, 2 * bs)
            right = field[pl.ds(f * bs, 2 * bs), pl.ds(at, 2 * bs)]
            square[pl.ds(a0 * bs, (a1 - a0) * bs), pl.ds(at, 2 * bs)] += jnp.dot(
                left, right, preferred_element_type=jnp.float32
            )
            return 0

        lax.fori_loop(0, (c1 - c0) // 2, body, 0)

    def second_hop(k):
        for way in range(2):
            x_copy(k, way).wait_recv()
            y_copy(k, way).start()

    def landed(f):
        for k in range(len(halo)):
            if halo[k][0] in (f, f + 1):
                for way in range(2):
                    y_copy(k, way).wait_recv()

    work = {}
    for p in range(rows // 2):
        work[p] = HB + 2 * p
    for p in range(HB // 2):
        work[5 + 4 * p] = HB - 2 - 2 * p
        work[6 + 4 * p] = HB + rows + 2 * p

    for t in range(7 + 4 * (HB // 2)):
        if t < len(halo):
            z_copy(t).wait_recv()
            for way in range(2):
                x_copy(t, way).start()
        if 1 <= t <= len(halo):
            second_hop(t - 1)
        if t in work:
            f = work[t]
            if t == 0:
                for copy in own_copies:
                    copy.wait()
            if not HB <= f < HB + rows:
                landed(f)
            add_pair(f)

    for k in range(len(halo)):
        z_copy(k).wait_send()
        for way in range(2):
            x_copy(k, way).wait_send()
            y_copy(k, way).wait_send()


def cube_kernel(off_ref, field, square, out_ref):
    rows, quarter, bs = out_ref.shape[:3]
    d = lax.axis_index("depth")
    slots = off_ref.shape[1]

    def cube_row(m, _):
        at = [pl.multiple_of((m + off_ref[m, s]) * bs, bs) for s in range(slots)]
        row = pl.ds(pl.multiple_of(m * bs, bs), bs)
        left = jnp.concatenate(
            [square[row, pl.ds(at[s], bs)].astype(field.dtype) for s in range(slots)], axis=1
        )
        for j in range(0, quarter, 2):
            to = [pl.multiple_of((m + off_ref[m, d * quarter + j + e]) * bs, bs) for e in range(2)]
            right = jnp.concatenate(
                [
                    jnp.concatenate([field[pl.ds(at[s], bs), pl.ds(to[e], bs)] for e in range(2)], axis=1)
                    for s in range(slots)
                ],
                axis=0,
            )
            cube = jnp.dot(left, right, preferred_element_type=jnp.float32)
            for e in range(2):
                out_ref[m, j + e] = (
                    3.0 * square[row, pl.ds(to[e], bs)] - 2.0 * cube[:, e * bs : (e + 1) * bs]
                ).astype(out_ref.dtype)
        return 0

    lax.fori_loop(0, rows, cube_row, 0)


def local(sizes, values, columns):
    rows, slots, bs, _ = values.shape
    total = columns.shape[0]
    layers = sizes[2]
    first = lax.axis_index(("row", "col")) * rows
    own_cols = lax.dynamic_slice_in_dim(columns, first, rows, 0)
    row_ids = first + jnp.arange(rows, dtype=jnp.int32)[:, None]
    off = jnp.mod(own_cols - row_ids + HB, total)
    own = spread(off, values)
    frame = rows + 2 * HB
    count = 2 * HB
    dma = pltpu.SemaphoreType.DMA
    vmem = pl.BlockSpec(memory_space=pltpu.VMEM)
    field, square = pl.pallas_call(
        functools.partial(square_kernel, sizes),
        out_shape=(
            pltpu.VMEM((frame * bs, frame * bs), values.dtype),
            pltpu.VMEM((rows * bs, frame * bs), jnp.float32),
        ),
        in_specs=[pl.BlockSpec(memory_space=pl.ANY)],
        out_specs=(vmem, vmem),
        scratch_shapes=[
            dma((rows,)),
            dma((count,)),
            dma((count,)),
            dma((2, count)),
            dma((2, count)),
            dma((2, count)),
            dma((2, count)),
        ],
        compiler_params=pltpu.CompilerParams(
            collective_id=0, has_side_effects=True, vmem_limit_bytes=4 * 1024 * 1024
        ),
    )(own)
    return pl.pallas_call(
        cube_kernel,
        out_shape=jax.ShapeDtypeStruct((rows, slots // layers, bs, bs), values.dtype),
        in_specs=[pl.BlockSpec(memory_space=pltpu.SMEM), vmem, vmem],
        out_specs=vmem,
        compiler_params=pltpu.CompilerParams(vmem_limit_bytes=4 * 1024 * 1024),
    )(off, field, square)


def solution(mesh):
    sizes = (mesh.shape["row"], mesh.shape["col"], mesh.shape["depth"])
    return jax.shard_map(
        functools.partial(local, sizes),
        mesh=mesh,
        in_specs=(P(("row", "col"), None, None, None), P()),
        out_specs=P(("row", "col"), "depth", None, None),
        check_vma=False,
    )
```

```python
import functools

import jax
import jax.numpy as jnp
from jax import lax
from jax.experimental import pallas as pl
from jax.experimental.pallas import tpu as pltpu
from jax.sharding import PartitionSpec as P

HB = 8
BAND = 2 * HB + 1
MESH = pl.DeviceIdType.MESH


def spread_kernel(off_ref, v_ref, o_ref, sem):
    rows, slots, bs = v_ref.shape[:3]

    def block(m, at):
        return o_ref.at[m, :, pl.ds(pl.multiple_of(at * bs, bs), bs)]

    def copy(m, s):
        return pltpu.make_async_copy(v_ref.at[m, s], block(m, off_ref[m, s]), sem.at[m, s])

    for m in range(rows):
        for s in range(slots):
            copy(m, s).start()
    for m in range(rows):
        absent = BAND * (BAND - 1) // 2
        for s in range(slots):
            absent = absent - off_ref[m, s]
        at = pl.multiple_of(absent * bs, bs)
        o_ref[m, :, pl.ds(at, bs)] = jnp.zeros((bs, bs), o_ref.dtype)
    for m in range(rows):
        for s in range(slots):
            copy(m, s).wait()


def spread(off, values):
    rows, slots, bs, _ = values.shape
    assert slots == BAND - 1
    return pl.pallas_call(
        spread_kernel,
        out_shape=pltpu.VMEM((rows, bs, BAND * bs), values.dtype),
        in_specs=[
            pl.BlockSpec(memory_space=pltpu.SMEM),
            pl.BlockSpec(memory_space=pltpu.HBM),
        ],
        out_specs=pl.BlockSpec(memory_space=pltpu.VMEM),
        scratch_shapes=[pltpu.SemaphoreType.DMA((rows, slots))],
        compiler_params=pltpu.CompilerParams(vmem_limit_bytes=58 * 1024 * 1024),
    )(off, values)


def halo_rows(rows):
    frame = rows + 2 * HB
    listed = []
    for near in range(HB):
        for f in (HB - 1 - near, HB + rows + near):
            owner, m = (f - HB) // rows, (f - HB) % rows
            lo = max(0, HB - f)
            hi = min(2 * HB, frame - 1 + HB - f)
            listed.append((f, owner, m, lo, f + lo - HB, hi - lo + 1))
    return listed


def square_kernel(sizes, own_ref, field, square, z_send, z_recv, w_send, w_recv, x_send, x_recv, y_send, y_recv):
    nrow, ncol, layers = sizes
    rows, bs = own_ref.shape[0], own_ref.shape[1]
    frame = rows + 2 * HB
    groups = nrow * ncol
    strip = bs // layers
    half = strip // 2
    r, c, d = lax.axis_index("row"), lax.axis_index("col"), lax.axis_index("depth")
    g = r * ncol + c
    halo = halo_rows(rows)

    def group_at(by):
        t = lax.rem(g + by + groups, groups)
        return (lax.div(t, ncol), lax.rem(t, ncol), d)

    up, down = lax.rem(d + 1, layers), lax.rem(d + layers - 1, layers)
    beside = ((r, c, up), (r, c, down))
    straight = (8, 9, 10, 11)
    reach = sorted({h[1] for h in halo if abs(h[1]) == 1})

    barrier = pltpu.get_barrier_semaphore()
    for by in reach:
        pl.semaphore_signal(barrier, inc=1, device_id=group_at(by), device_id_type=MESH)
    for peer in beside:
        pl.semaphore_signal(barrier, inc=1, device_id=peer, device_id_type=MESH)
    pl.semaphore_wait(barrier, len(reach) + 2)

    def part(k, layer, start, count):
        f, _, _, _, col, blocks = halo[k]
        first = pl.multiple_of(f * bs + layer * strip + start, half)
        return field.at[pl.ds(first, count), pl.ds(col * bs, blocks * bs)]

    def z_copy(k):
        f, owner, m, lo, col, blocks = halo[k]
        step = 1 if owner > 0 else -1
        if owner == step:
            rows_at = pl.ds(pl.multiple_of(d * strip, strip), strip)
            src = own_ref.at[m, rows_at, pl.ds(lo * bs, blocks * bs)]
        else:
            first = pl.multiple_of((f - step * rows) * bs + d * strip, half)
            src = field.at[pl.ds(first, strip), pl.ds((col - step * rows) * bs, blocks * bs)]
        return pltpu.make_async_remote_copy(
            src, part(k, d, 0, strip), z_send.at[k], z_recv.at[k], group_at(-step), MESH
        )

    def w_copy(k):
        f, owner, m, lo, col, blocks = halo[k]
        q = lax.rem(d + layers // 2, layers)
        rows_at = pl.ds(pl.multiple_of(q * strip, strip), strip)
        src = own_ref.at[m, rows_at, pl.ds(lo * bs, blocks * bs)]
        return pltpu.make_async_remote_copy(
            src, part(k, q, 0, strip), w_send.at[k], w_recv.at[k], group_at(-owner), MESH
        )

    def relays(k):
        f, owner = halo[k][:2]
        for j in range(len(halo)):
            if halo[j][1] == 2 * owner and halo[j][0] == f + owner * rows:
                z_copy(j).start()

    def x_copy(k, way):
        ref = part(k, d, 0, strip)
        return pltpu.make_async_remote_copy(ref, ref, x_send.at[way, k], x_recv.at[way, k], beside[way], MESH)

    def y_copy(k, way):
        ref = part(k, (down, up)[way], way * half, half)
        return pltpu.make_async_remote_copy(ref, ref, y_send.at[way, k], y_recv.at[way, k], beside[way], MESH)

    for k in range(len(halo)):
        if abs(halo[k][1]) == 1:
            z_copy(k).start()

    def clear(f):
        low, high = max(0, f - HB), min(frame, f + HB + 1)
        if low:
            field[pl.ds(f * bs, bs), pl.ds(0, low * bs)] = jnp.zeros((bs, low * bs), field.dtype)
        if high < frame:
            field[pl.ds(f * bs, bs), pl.ds(high * bs, (frame - high) * bs)] = jnp.zeros(
                (bs, (frame - high) * bs), field.dtype
            )

    def place_own():
        for m in range(rows):
            field[pl.ds((HB + m) * bs, bs), pl.ds(m * bs, BAND * bs)] = own_ref[m]
            clear(HB + m)
        done = 2 * HB + 2
        square[:, pl.ds(done * bs, (frame - done) * bs)] = jnp.zeros(
            (rows * bs, (frame - done) * bs), square.dtype
        )

    def add_pair(f):
        a0, a1 = max(0, f - 2 * HB), min(rows, f + 2)
        c0, c1 = max(0, f - HB), min(frame, f + HB + 2)
        left = field[pl.ds((HB + a0) * bs, (a1 - a0) * bs), pl.ds(f * bs, 2 * bs)]

        def body(t, _):
            at = pl.multiple_of((c0 + 2 * t) * bs, 2 * bs)
            right = field[pl.ds(f * bs, 2 * bs), pl.ds(at, 2 * bs)]
            term = jnp.dot(left, right, preferred_element_type=jnp.float32)
            to = pl.ds(a0 * bs, (a1 - a0) * bs), pl.ds(at, 2 * bs)
            if f == HB:
                square[to] = term
            else:
                square[to] += term
            return 0

        lax.fori_loop(0, (c1 - c0) // 2, body, 0)

    def second_hop(k):
        for way in range(2):
            x_copy(k, way).wait_recv()
            if k not in straight:
                y_copy(k, way).start()

    def landed(f):
        for k in range(len(halo)):
            if halo[k][0] in (f, f + 1):
                if k in straight:
                    w_copy(k).wait_recv()
                    continue
                for way in range(2):
                    y_copy(k, way).wait_recv()

    lag = 2
    work = {p: HB + 2 * p for p in range(rows // 2)}
    for p in range(HB // 2):
        work[6 + 4 * p] = HB - 2 - 2 * p
        work[7 + 4 * p] = HB + rows + 2 * p

    for t in range(8 + 4 * (HB // 2)):
        if t < len(halo):
            z_copy(t).wait_recv()
            for way in range(2):
                x_copy(t, way).start()
            relays(t)
            if t == 3:
                for k in straight:
                    w_copy(k).start()
        if lag <= t < len(halo) + lag:
            second_hop(t - lag)
        if t == 0:
            place_own()
        if 1 <= t <= HB // 2:
            for f in (2 * t - 2, 2 * t - 1):
                clear(f)
                clear(HB + rows + f)
        if t in work:
            f = work[t]
            if not HB <= f < HB + rows:
                landed(f)
            add_pair(f)

    for k in range(len(halo)):
        z_copy(k).wait_send()
        for way in range(2):
            x_copy(k, way).wait_send()
            if k not in straight:
                y_copy(k, way).wait_send()
        if k in straight:
            w_copy(k).wait_send()


def cube_kernel(off_ref, field, square, out_ref):
    rows, quarter, bs = out_ref.shape[:3]
    d = lax.axis_index("depth")
    slots = off_ref.shape[1]

    def cube_row(m, _):
        at = [pl.multiple_of((m + off_ref[m, s]) * bs, bs) for s in range(slots)]
        row = pl.ds(pl.multiple_of(m * bs, bs), bs)
        left = jnp.concatenate(
            [square[row, pl.ds(at[s], bs)].astype(field.dtype) for s in range(slots)], axis=1
        )
        for j in range(0, quarter, 2):
            to = [pl.multiple_of((m + off_ref[m, d * quarter + j + e]) * bs, bs) for e in range(2)]
            right = jnp.concatenate(
                [
                    jnp.concatenate([field[pl.ds(at[s], bs), pl.ds(to[e], bs)] for e in range(2)], axis=1)
                    for s in range(slots)
                ],
                axis=0,
            )
            cube = jnp.dot(left, right, preferred_element_type=jnp.float32)
            for e in range(2):
                out_ref[m, j + e] = (
                    3.0 * square[row, pl.ds(to[e], bs)] - 2.0 * cube[:, e * bs : (e + 1) * bs]
                ).astype(out_ref.dtype)
        return 0

    lax.fori_loop(0, rows, cube_row, 0)


def local(sizes, values, columns):
    rows, slots, bs, _ = values.shape
    total = columns.shape[0]
    layers = sizes[2]
    first = lax.axis_index(("row", "col")) * rows
    own_cols = lax.dynamic_slice_in_dim(columns, first, rows, 0)
    row_ids = first + jnp.arange(rows, dtype=jnp.int32)[:, None]
    off = jnp.mod(own_cols - row_ids + HB, total)
    own = spread(off, values)
    frame = rows + 2 * HB
    count = 2 * HB
    dma = pltpu.SemaphoreType.DMA
    vmem = pl.BlockSpec(memory_space=pltpu.VMEM)
    field, square = pl.pallas_call(
        functools.partial(square_kernel, sizes),
        out_shape=(
            pltpu.VMEM((frame * bs, frame * bs), values.dtype),
            pltpu.VMEM((rows * bs, frame * bs), jnp.float32),
        ),
        in_specs=[vmem],
        out_specs=(vmem, vmem),
        scratch_shapes=[
            dma((count,)),
            dma((count,)),
            dma((count,)),
            dma((count,)),
            dma((2, count)),
            dma((2, count)),
            dma((2, count)),
            dma((2, count)),
        ],
        compiler_params=pltpu.CompilerParams(
            collective_id=0, has_side_effects=True, vmem_limit_bytes=4 * 1024 * 1024
        ),
    )(own)
    return pl.pallas_call(
        cube_kernel,
        out_shape=jax.ShapeDtypeStruct((rows, slots // layers, bs, bs), values.dtype),
        in_specs=[pl.BlockSpec(memory_space=pltpu.SMEM), vmem, vmem],
        out_specs=vmem,
        compiler_params=pltpu.CompilerParams(vmem_limit_bytes=4 * 1024 * 1024),
    )(off, field, square)


def solution(mesh):
    sizes = (mesh.shape["row"], mesh.shape["col"], mesh.shape["depth"])
    return jax.shard_map(
        functools.partial(local, sizes),
        mesh=mesh,
        in_specs=(P(("row", "col"), None, None, None), P()),
        out_specs=P(("row", "col"), "depth", None, None),
        check_vma=False,
    )
```

```python
import functools

import jax
import jax.numpy as jnp
from jax import lax
from jax.experimental import pallas as pl
from jax.experimental.pallas import tpu as pltpu
from jax.sharding import PartitionSpec as P

HB = 8
BAND = 2 * HB + 1
MESH = pl.DeviceIdType.MESH


def spread_kernel(off_ref, v_ref, o_ref, sem):
    rows, slots, bs = v_ref.shape[:3]

    def block(m, at):
        return o_ref.at[m, :, pl.ds(pl.multiple_of(at * bs, bs), bs)]

    def copy(m, s):
        return pltpu.make_async_copy(v_ref.at[m, s], block(m, off_ref[m, s]), sem.at[m, s])

    for m in range(rows):
        for s in range(slots):
            copy(m, s).start()
    for m in range(rows):
        absent = BAND * (BAND - 1) // 2
        for s in range(slots):
            absent = absent - off_ref[m, s]
        at = pl.multiple_of(absent * bs, bs)
        o_ref[m, :, pl.ds(at, bs)] = jnp.zeros((bs, bs), o_ref.dtype)
    for m in range(rows):
        for s in range(slots):
            copy(m, s).wait()


def spread(off, values):
    rows, slots, bs, _ = values.shape
    assert slots == BAND - 1
    return pl.pallas_call(
        spread_kernel,
        out_shape=pltpu.VMEM((rows, bs, BAND * bs), values.dtype),
        in_specs=[
            pl.BlockSpec(memory_space=pltpu.SMEM),
            pl.BlockSpec(memory_space=pltpu.HBM),
        ],
        out_specs=pl.BlockSpec(memory_space=pltpu.VMEM),
        scratch_shapes=[pltpu.SemaphoreType.DMA((rows, slots))],
        compiler_params=pltpu.CompilerParams(vmem_limit_bytes=58 * 1024 * 1024),
    )(off, values)


def halo_rows(rows):
    frame = rows + 2 * HB
    listed = []
    for near in (*range(HB - 4), HB - 2, HB - 1, HB - 4, HB - 3):
        for f in (HB - 1 - near, HB + rows + near):
            owner, m = (f - HB) // rows, (f - HB) % rows
            lo = max(0, HB - f)
            hi = min(2 * HB, frame - 1 + HB - f)
            listed.append((f, owner, m, lo, f + lo - HB, hi - lo + 1))
    return listed


def square_kernel(sizes, own_ref, field, square, z_send, z_recv, w_send, w_recv, x_send, x_recv, y_send, y_recv):
    nrow, ncol, layers = sizes
    rows, bs = own_ref.shape[0], own_ref.shape[1]
    frame = rows + 2 * HB
    groups = nrow * ncol
    strip = bs // layers
    half = strip // 2
    r, c, d = lax.axis_index("row"), lax.axis_index("col"), lax.axis_index("depth")
    g = r * ncol + c
    halo = halo_rows(rows)

    def group_at(by):
        t = lax.rem(g + by + groups, groups)
        return (lax.div(t, ncol), lax.rem(t, ncol), d)

    up, down = lax.rem(d + 1, layers), lax.rem(d + layers - 1, layers)
    beside = ((r, c, up), (r, c, down))
    straight = tuple(range(len(halo) - 4, len(halo)))
    reach = sorted({h[1] for h in halo if abs(h[1]) == 1})

    barrier = pltpu.get_barrier_semaphore()
    for by in reach:
        pl.semaphore_signal(barrier, inc=1, device_id=group_at(by), device_id_type=MESH)
    for peer in beside:
        pl.semaphore_signal(barrier, inc=1, device_id=peer, device_id_type=MESH)
    pl.semaphore_wait(barrier, len(reach) + 2)

    def part(k, layer, start, count):
        f, _, _, _, col, blocks = halo[k]
        first = pl.multiple_of(f * bs + layer * strip + start, half)
        return field.at[pl.ds(first, count), pl.ds(col * bs, blocks * bs)]

    def z_copy(k):
        f, owner, m, lo, col, blocks = halo[k]
        step = 1 if owner > 0 else -1
        if owner == step:
            rows_at = pl.ds(pl.multiple_of(d * strip, strip), strip)
            src = own_ref.at[m, rows_at, pl.ds(lo * bs, blocks * bs)]
        else:
            first = pl.multiple_of((f - step * rows) * bs + d * strip, half)
            src = field.at[pl.ds(first, strip), pl.ds((col - step * rows) * bs, blocks * bs)]
        return pltpu.make_async_remote_copy(
            src, part(k, d, 0, strip), z_send.at[k], z_recv.at[k], group_at(-step), MESH
        )

    def w_copy(k):
        f, owner, m, lo, col, blocks = halo[k]
        q = lax.rem(d + layers // 2, layers)
        rows_at = pl.ds(pl.multiple_of(q * strip, strip), strip)
        src = own_ref.at[m, rows_at, pl.ds(lo * bs, blocks * bs)]
        return pltpu.make_async_remote_copy(
            src, part(k, q, 0, strip), w_send.at[k], w_recv.at[k], group_at(-owner), MESH
        )

    def relays(k):
        f, owner = halo[k][:2]
        for j in range(len(halo)):
            if halo[j][1] == 2 * owner and halo[j][0] == f + owner * rows:
                z_copy(j).start()

    def x_copy(k, way):
        ref = part(k, d, 0, strip)
        return pltpu.make_async_remote_copy(ref, ref, x_send.at[way, k], x_recv.at[way, k], beside[way], MESH)

    def y_copy(k, way):
        ref = part(k, (down, up)[way], way * half, half)
        return pltpu.make_async_remote_copy(ref, ref, y_send.at[way, k], y_recv.at[way, k], beside[way], MESH)

    for k in range(len(halo)):
        if abs(halo[k][1]) == 1 and k not in straight:
            z_copy(k).start()

    def clear(f):
        low, high = max(0, f - HB), min(frame, f + HB + 1)
        if low:
            field[pl.ds(f * bs, bs), pl.ds(0, low * bs)] = jnp.zeros((bs, low * bs), field.dtype)
        if high < frame:
            field[pl.ds(f * bs, bs), pl.ds(high * bs, (frame - high) * bs)] = jnp.zeros(
                (bs, (frame - high) * bs), field.dtype
            )

    def place_own():
        for m in range(rows):
            field[pl.ds((HB + m) * bs, bs), pl.ds(m * bs, BAND * bs)] = own_ref[m]
            clear(HB + m)
        done = 2 * HB + 2
        square[:, pl.ds(done * bs, (frame - done) * bs)] = jnp.zeros(
            (rows * bs, (frame - done) * bs), square.dtype
        )

    def add_pair(f):
        a0, a1 = max(0, f - 2 * HB), min(rows, f + 2)
        c0, c1 = max(0, f - HB), min(frame, f + HB + 2)
        left = field[pl.ds((HB + a0) * bs, (a1 - a0) * bs), pl.ds(f * bs, 2 * bs)]

        def body(t, _):
            at = pl.multiple_of((c0 + 2 * t) * bs, 2 * bs)
            right = field[pl.ds(f * bs, 2 * bs), pl.ds(at, 2 * bs)]
            term = jnp.dot(left, right, preferred_element_type=jnp.float32)
            to = pl.ds(a0 * bs, (a1 - a0) * bs), pl.ds(at, 2 * bs)
            if f == HB:
                square[to] = term
            else:
                square[to] += term
            return 0

        lax.fori_loop(0, (c1 - c0) // 2, body, 0)

    def second_hop(k):
        for way in range(2):
            x_copy(k, way).wait_recv()
            if k not in straight:
                y_copy(k, way).start()

    def landed(f):
        for k in range(len(halo)):
            if halo[k][0] in (f, f + 1):
                if k in straight:
                    w_copy(k).wait_recv()
                    continue
                for way in range(2):
                    y_copy(k, way).wait_recv()

    lag = 2
    work = {p: HB + 2 * p for p in range(rows // 2)}
    for p, t in zip((0, 1, 3, 2), (6, 10, 14, 17)):
        work[t] = HB - 2 - 2 * p
        work[t + 1] = HB + rows + 2 * p

    for t in range(len(halo) + 3):
        if t < len(halo):
            z_copy(t).wait_recv()
            for way in range(2):
                x_copy(t, way).start()
            relays(t)
            if t == 3:
                for k in straight:
                    z_copy(k).start()
                for k in straight:
                    w_copy(k).start()
        if lag <= t < len(halo) + lag:
            second_hop(t - lag)
        if t == 0:
            place_own()
        if 1 <= t <= HB // 2:
            for f in (2 * t - 2, 2 * t - 1):
                clear(f)
                clear(HB + rows + f)
        if t in work:
            f = work[t]
            if not HB <= f < HB + rows:
                landed(f)
            add_pair(f)

    for k in range(len(halo)):
        z_copy(k).wait_send()
        for way in range(2):
            x_copy(k, way).wait_send()
            if k not in straight:
                y_copy(k, way).wait_send()
        if k in straight:
            w_copy(k).wait_send()


def cube_kernel(off_ref, field, square, out_ref):
    rows, quarter, bs = out_ref.shape[:3]
    d = lax.axis_index("depth")
    slots = off_ref.shape[1]

    def cube_row(m, _):
        at = [pl.multiple_of((m + off_ref[m, s]) * bs, bs) for s in range(slots)]
        row = pl.ds(pl.multiple_of(m * bs, bs), bs)
        left = jnp.concatenate(
            [square[row, pl.ds(at[s], bs)].astype(field.dtype) for s in range(slots)], axis=1
        )
        for j in range(0, quarter, 2):
            to = [pl.multiple_of((m + off_ref[m, d * quarter + j + e]) * bs, bs) for e in range(2)]
            right = jnp.concatenate(
                [
                    jnp.concatenate([field[pl.ds(at[s], bs), pl.ds(to[e], bs)] for e in range(2)], axis=1)
                    for s in range(slots)
                ],
                axis=0,
            )
            cube = jnp.dot(left, right, preferred_element_type=jnp.float32)
            for e in range(2):
                out_ref[m, j + e] = (
                    3.0 * square[row, pl.ds(to[e], bs)] - 2.0 * cube[:, e * bs : (e + 1) * bs]
                ).astype(out_ref.dtype)
        return 0

    lax.fori_loop(0, rows, cube_row, 0)


def local(sizes, values, columns):
    rows, slots, bs, _ = values.shape
    total = columns.shape[0]
    layers = sizes[2]
    first = lax.axis_index(("row", "col")) * rows
    own_cols = lax.dynamic_slice_in_dim(columns, first, rows, 0)
    row_ids = first + jnp.arange(rows, dtype=jnp.int32)[:, None]
    off = jnp.mod(own_cols - row_ids + HB, total)
    own = spread(off, values)
    frame = rows + 2 * HB
    count = 2 * HB
    dma = pltpu.SemaphoreType.DMA
    vmem = pl.BlockSpec(memory_space=pltpu.VMEM)
    field, square = pl.pallas_call(
        functools.partial(square_kernel, sizes),
        out_shape=(
            pltpu.VMEM((frame * bs, frame * bs), values.dtype),
            pltpu.VMEM((rows * bs, frame * bs), jnp.float32),
        ),
        in_specs=[vmem],
        out_specs=(vmem, vmem),
        scratch_shapes=[
            dma((count,)),
            dma((count,)),
            dma((count,)),
            dma((count,)),
            dma((2, count)),
            dma((2, count)),
            dma((2, count)),
            dma((2, count)),
        ],
        compiler_params=pltpu.CompilerParams(
            collective_id=0, has_side_effects=True, vmem_limit_bytes=4 * 1024 * 1024
        ),
    )(own)
    return pl.pallas_call(
        cube_kernel,
        out_shape=jax.ShapeDtypeStruct((rows, slots // layers, bs, bs), values.dtype),
        in_specs=[pl.BlockSpec(memory_space=pltpu.SMEM), vmem, vmem],
        out_specs=vmem,
        compiler_params=pltpu.CompilerParams(vmem_limit_bytes=4 * 1024 * 1024),
    )(off, field, square)


def solution(mesh):
    sizes = (mesh.shape["row"], mesh.shape["col"], mesh.shape["depth"])
    return jax.shard_map(
        functools.partial(local, sizes),
        mesh=mesh,
        in_specs=(P(("row", "col"), None, None, None), P()),
        out_specs=P(("row", "col"), "depth", None, None),
        check_vma=False,
    )
```

```python
import functools

import jax
import jax.numpy as jnp
from jax import lax
from jax.experimental import pallas as pl
from jax.experimental.pallas import tpu as pltpu
from jax.sharding import PartitionSpec as P

HB = 8
BAND = 2 * HB + 1
MESH = pl.DeviceIdType.MESH


def spread_kernel(off_ref, v_ref, o_ref, sem):
    rows, slots, bs = v_ref.shape[:3]

    def block(m, at):
        return o_ref.at[m, :, pl.ds(pl.multiple_of(at * bs, bs), bs)]

    def copy(m, s):
        return pltpu.make_async_copy(v_ref.at[m, s], block(m, off_ref[m, s]), sem.at[m, s])

    for m in range(rows):
        for s in range(slots):
            copy(m, s).start()
    for m in range(rows):
        absent = BAND * (BAND - 1) // 2
        for s in range(slots):
            absent = absent - off_ref[m, s]
        at = pl.multiple_of(absent * bs, bs)
        o_ref[m, :, pl.ds(at, bs)] = jnp.zeros((bs, bs), o_ref.dtype)
    for m in range(rows):
        for s in range(slots):
            copy(m, s).wait()


def spread(off, values):
    rows, slots, bs, _ = values.shape
    assert slots == BAND - 1
    return pl.pallas_call(
        spread_kernel,
        out_shape=pltpu.VMEM((rows, bs, BAND * bs), values.dtype),
        in_specs=[
            pl.BlockSpec(memory_space=pltpu.SMEM),
            pl.BlockSpec(memory_space=pltpu.HBM),
        ],
        out_specs=pl.BlockSpec(memory_space=pltpu.VMEM),
        scratch_shapes=[pltpu.SemaphoreType.DMA((rows, slots))],
        compiler_params=pltpu.CompilerParams(vmem_limit_bytes=58 * 1024 * 1024),
    )(off, values)


def halo_rows(rows):
    frame = rows + 2 * HB
    listed = []
    for near in (*range(HB - 4), HB - 2, HB - 1, HB - 4, HB - 3):
        for f in (HB - 1 - near, HB + rows + near):
            owner, m = (f - HB) // rows, (f - HB) % rows
            lo = max(0, HB - f)
            hi = min(2 * HB, frame - 1 + HB - f)
            listed.append((f, owner, m, lo, f + lo - HB, hi - lo + 1))
    return listed


def square_kernel(sizes, own_ref, field, square, z_send, z_recv, w_send, w_recv, x_send, x_recv, y_send, y_recv):
    nrow, ncol, layers = sizes
    rows, bs = own_ref.shape[0], own_ref.shape[1]
    frame = rows + 2 * HB
    groups = nrow * ncol
    strip = bs // layers
    half = strip // 2
    r, c, d = lax.axis_index("row"), lax.axis_index("col"), lax.axis_index("depth")
    g = r * ncol + c
    halo = halo_rows(rows)

    def group_at(by):
        t = lax.rem(g + by + groups, groups)
        return (lax.div(t, ncol), lax.rem(t, ncol), d)

    up, down = lax.rem(d + 1, layers), lax.rem(d + layers - 1, layers)
    beside = ((r, c, up), (r, c, down))
    straight = tuple(range(len(halo) - 4, len(halo)))
    reach = sorted({h[1] for h in halo if abs(h[1]) == 1})

    barrier = pltpu.get_barrier_semaphore()
    for by in reach:
        pl.semaphore_signal(barrier, inc=1, device_id=group_at(by), device_id_type=MESH)
    for peer in beside:
        pl.semaphore_signal(barrier, inc=1, device_id=peer, device_id_type=MESH)
    pl.semaphore_wait(barrier, len(reach) + 2)

    def part(k, layer, start, count):
        f, _, _, _, col, blocks = halo[k]
        first = pl.multiple_of(f * bs + layer * strip + start, half)
        return field.at[pl.ds(first, count), pl.ds(col * bs, blocks * bs)]

    def z_copy(k):
        f, owner, m, lo, col, blocks = halo[k]
        step = 1 if owner > 0 else -1
        if owner == step:
            rows_at = pl.ds(pl.multiple_of(d * strip, strip), strip)
            src = own_ref.at[m, rows_at, pl.ds(lo * bs, blocks * bs)]
        else:
            first = pl.multiple_of((f - step * rows) * bs + d * strip, half)
            src = field.at[pl.ds(first, strip), pl.ds((col - step * rows) * bs, blocks * bs)]
        return pltpu.make_async_remote_copy(
            src, part(k, d, 0, strip), z_send.at[k], z_recv.at[k], group_at(-step), MESH
        )

    def w_copy(k):
        f, owner, m, lo, col, blocks = halo[k]
        q = lax.rem(d + layers // 2, layers)
        rows_at = pl.ds(pl.multiple_of(q * strip, strip), strip)
        src = own_ref.at[m, rows_at, pl.ds(lo * bs, blocks * bs)]
        return pltpu.make_async_remote_copy(
            src, part(k, q, 0, strip), w_send.at[k], w_recv.at[k], group_at(-owner), MESH
        )

    def relays(k):
        f, owner = halo[k][:2]
        for j in range(len(halo)):
            if halo[j][1] == 2 * owner and halo[j][0] == f + owner * rows:
                z_copy(j).start()

    def x_copy(k, way):
        ref = part(k, d, 0, strip)
        return pltpu.make_async_remote_copy(ref, ref, x_send.at[way, k], x_recv.at[way, k], beside[way], MESH)

    def y_copy(k, way):
        ref = part(k, (down, up)[way], way * half, half)
        return pltpu.make_async_remote_copy(ref, ref, y_send.at[way, k], y_recv.at[way, k], beside[way], MESH)

    for k in range(len(halo)):
        if abs(halo[k][1]) == 1 and k not in straight:
            z_copy(k).start()

    def clear(f):
        low, high = max(0, f - HB), min(frame, f + HB + 1)
        if low:
            field[pl.ds(f * bs, bs), pl.ds(0, low * bs)] = jnp.zeros((bs, low * bs), field.dtype)
        if high < frame:
            field[pl.ds(f * bs, bs), pl.ds(high * bs, (frame - high) * bs)] = jnp.zeros(
                (bs, (frame - high) * bs), field.dtype
            )

    def place_own():
        for m in range(rows):
            field[pl.ds((HB + m) * bs, bs), pl.ds(m * bs, BAND * bs)] = own_ref[m]
            clear(HB + m)
        done = 2 * HB + 2
        square[:, pl.ds(done * bs, (frame - done) * bs)] = jnp.zeros(
            (rows * bs, (frame - done) * bs), square.dtype
        )

    def add_pair(f):
        a0, a1 = max(0, f - 2 * HB), min(rows, f + 2)
        c0, c1 = max(0, f - HB), min(frame, f + HB + 2)
        left = field[pl.ds((HB + a0) * bs, (a1 - a0) * bs), pl.ds(f * bs, 2 * bs)]

        def body(t, _):
            at = pl.multiple_of((c0 + 2 * t) * bs, 2 * bs)
            right = field[pl.ds(f * bs, 2 * bs), pl.ds(at, 2 * bs)]
            term = jnp.dot(left, right, preferred_element_type=jnp.float32)
            to = pl.ds(a0 * bs, (a1 - a0) * bs), pl.ds(at, 2 * bs)
            if f == HB:
                square[to] = term
            else:
                square[to] += term
            return 0

        lax.fori_loop(0, (c1 - c0) // 2, body, 0)

    def second_hop(k):
        for way in range(2):
            x_copy(k, way).wait_recv()
            if k not in straight:
                y_copy(k, way).start()

    def landed(f):
        for k in range(len(halo)):
            if halo[k][0] in (f, f + 1):
                if k in straight:
                    w_copy(k).wait_recv()
                    continue
                for way in range(2):
                    y_copy(k, way).wait_recv()

    lag = 3
    work = {1 + 2 * p: HB + 2 * p for p in range(rows // 2)}
    for p, t in zip((0, 1, 3, 2), ((9, 11), (15, 16), (17, 18), (19, 20))):
        work[t[0]] = HB - 2 - 2 * p
        work[t[1]] = HB + rows + 2 * p

    for t in range(len(halo) + 5):
        if t < len(halo):
            z_copy(t).wait_recv()
            for way in range(2):
                x_copy(t, way).start()
            relays(t)
            if t == 3:
                for k in straight:
                    z_copy(k).start()
                for k in straight:
                    w_copy(k).start()
        if lag <= t < len(halo) + lag:
            second_hop(t - lag)
        if t == 0:
            place_own()
        if 1 <= t <= HB // 2:
            for f in (2 * t - 2, 2 * t - 1):
                clear(f)
                clear(HB + rows + f)
        if t in work:
            f = work[t]
            if not HB <= f < HB + rows:
                landed(f)
            add_pair(f)

    for k in range(len(halo)):
        z_copy(k).wait_send()
        for way in range(2):
            x_copy(k, way).wait_send()
            if k not in straight:
                y_copy(k, way).wait_send()
        if k in straight:
            w_copy(k).wait_send()


def cube_kernel(off_ref, field, square, out_ref):
    rows, quarter, bs = out_ref.shape[:3]
    d = lax.axis_index("depth")
    slots = off_ref.shape[1]

    def cube_row(m, _):
        at = [pl.multiple_of((m + off_ref[m, s]) * bs, bs) for s in range(slots)]
        row = pl.ds(pl.multiple_of(m * bs, bs), bs)
        left = jnp.concatenate(
            [square[row, pl.ds(at[s], bs)].astype(field.dtype) for s in range(slots)], axis=1
        )
        for j in range(0, quarter, 2):
            to = [pl.multiple_of((m + off_ref[m, d * quarter + j + e]) * bs, bs) for e in range(2)]
            right = jnp.concatenate(
                [
                    jnp.concatenate([field[pl.ds(at[s], bs), pl.ds(to[e], bs)] for e in range(2)], axis=1)
                    for s in range(slots)
                ],
                axis=0,
            )
            cube = jnp.dot(left, right, preferred_element_type=jnp.float32)
            for e in range(2):
                out_ref[m, j + e] = (
                    3.0 * square[row, pl.ds(to[e], bs)] - 2.0 * cube[:, e * bs : (e + 1) * bs]
                ).astype(out_ref.dtype)
        return 0

    lax.fori_loop(0, rows, cube_row, 0)


def local(sizes, values, columns):
    rows, slots, bs, _ = values.shape
    total = columns.shape[0]
    layers = sizes[2]
    first = lax.axis_index(("row", "col")) * rows
    own_cols = lax.dynamic_slice_in_dim(columns, first, rows, 0)
    row_ids = first + jnp.arange(rows, dtype=jnp.int32)[:, None]
    off = jnp.mod(own_cols - row_ids + HB, total)
    own = spread(off, values)
    frame = rows + 2 * HB
    count = 2 * HB
    dma = pltpu.SemaphoreType.DMA
    vmem = pl.BlockSpec(memory_space=pltpu.VMEM)
    field, square = pl.pallas_call(
        functools.partial(square_kernel, sizes),
        out_shape=(
            pltpu.VMEM((frame * bs, frame * bs), values.dtype),
            pltpu.VMEM((rows * bs, frame * bs), jnp.float32),
        ),
        in_specs=[vmem],
        out_specs=(vmem, vmem),
        scratch_shapes=[
            dma((count,)),
            dma((count,)),
            dma((count,)),
            dma((count,)),
            dma((2, count)),
            dma((2, count)),
            dma((2, count)),
            dma((2, count)),
        ],
        compiler_params=pltpu.CompilerParams(
            collective_id=0, has_side_effects=True, vmem_limit_bytes=4 * 1024 * 1024
        ),
    )(own)
    return pl.pallas_call(
        cube_kernel,
        out_shape=jax.ShapeDtypeStruct((rows, slots // layers, bs, bs), values.dtype),
        in_specs=[pl.BlockSpec(memory_space=pltpu.SMEM), vmem, vmem],
        out_specs=vmem,
        compiler_params=pltpu.CompilerParams(vmem_limit_bytes=4 * 1024 * 1024),
    )(off, field, square)


def solution(mesh):
    sizes = (mesh.shape["row"], mesh.shape["col"], mesh.shape["depth"])
    return jax.shard_map(
        functools.partial(local, sizes),
        mesh=mesh,
        in_specs=(P(("row", "col"), None, None, None), P()),
        out_specs=P(("row", "col"), "depth", None, None),
        check_vma=False,
    )
```
